32 devices in a mesh: sec: 2 (over core), grp: 4 (over y, x), dev: 4 (over z).
Axes of the slice: x: 2, y: 2, z: 4, core: 2. Of those that a mesh axis runs over, the one named last changes fastest.
Arguments:
- current: float32 [32, 196608], P(None, ('sec', 'grp', 'dev')), may hold values from -6 to 6
- prior: float32 [8, 32, 196608], P(None, None, ('sec', 'grp', 'dev')), as said below
- block_values: float32 [1024, 6, 9216], P(('grp', 'dev')), may hold values from -0.25 to 0.25
- block_cols: int32 [1024, 6], P(('grp', 'dev')), may hold values from 0 to 63
- face_match: int32 [16, 4, 1536], P(('grp', 'dev')), may hold values from 0 to 1535, each once within a row
- face_weight: float32 [16, 4, 1536], P(('grp', 'dev')), may hold values from -3 to 3
- fluid_diag: float32 [98304], P(('grp', 'dev')), may hold values from 2 to 4
- wet_source: int32 [49152], P(('grp', 'dev')), may hold values from 0 to 6143
- wet_dest: int32 [49152, 1], P(('grp', 'dev')), may hold values from 0 to 15; in each aligned block of 3072 rows (0 to 3071, 3072 to 6143, ...) at most 392 rows name the same one
- wet_target: int32 [49152], P(('grp', 'dev')), may hold values from 0 to 6143
- wet_weight: float32 [49152], P(('grp', 'dev')), may hold values from -5 to 5
Outputs:
- next_block: float32 [32, 196608], P(None, ('sec', 'grp', 'dev'))
- coeffs: float32 [8, 32, 32], replicated
- rfac: float32 [32, 32], replicated
The draws below stay inside these ranges and needn't reach their ends.
Inputs may be any that keep to these rules, and one draw needn't show every extreme that they name: `block_cols`: block columns index blocks within the same subdomain. `face_match`: each subdomain's matching of one round is a permutation of its face. `prior`: each earlier block's columns have about unit length. `wet_dest`: among one structure subdomain's couplings, at most 392 name the same fluid subdomain, and some subdomain has exactly 392 for one.
All inputs are finite; a program needn't handle non-finite values.
Results may differ from the reference program's by a relative error of at most 0.00008.
Values sent between devices are 32-bit elements; how exact they have to be, the bound alone decides.
A program may use at most 128 MiB of HBM per device.

```python
import math
import jax
import jax.numpy as jnp
import numpy as np
from jax import lax

K = 32
NPRIOR = 8
BS = 96
RB = 64
NB = 6
ROUNDS = 4
R = 6144
FACE = 1536
WS = 3072
P_SIZE = 16
CAP = 392
ROWS = 196608
N_GRP = 4
N_DEV = 4


def draw_prior(key, part):
    first_key = jax.random.fold_in(key, 11)
    second_key = jax.random.fold_in(key, 12)
    fresh = jax.random.truncated_normal(first_key, -4.0, 4.0, (NPRIOR, K, ROWS), jnp.float32)
    shared = jax.random.truncated_normal(second_key, -4.0, 4.0, (1, K, ROWS), jnp.float32)
    return (fresh + 0.5 * shared) * (1.0 / math.sqrt(1.25 * ROWS))


def plant(entries, key, least, top_value):
    shape = entries.shape
    spot = [jax.random.randint(jax.random.fold_in(key, axis), (), 0, shape[axis]) for axis in range(len(shape))]
    entries = entries.at[tuple(spot)].set(least)
    longest = shape.index(max(shape))
    spot[longest] = (spot[longest] + 1) % shape[longest]
    return entries.at[tuple(spot)].set(top_value)


def steps_of(rng, shape, shards, least, largest):
    loudness = 1.0
    for axis_at, shards_of in shards:
        steps = jax.random.uniform(jax.random.fold_in(jax.random.fold_in(rng, 6), axis_at), (shards_of,), jnp.float32, least / len(shards), largest / len(shards))
        loudness = loudness * jnp.repeat(jnp.exp(steps), shape[axis_at] // shards_of).reshape((-1,) + (1,) * (len(shape) - 1 - axis_at))
    return loudness


def shared_out(key, own, number, rows, amount, top, limit, lean):
    order = jax.random.permutation(key, amount)
    crowded, common = shares(amount, rows * top, limit, lean, True), shares(amount, rows * top, limit, lean, False)
    places = jnp.arange(amount)

    def named(sizes, offset_by):
        used = int((sizes > 0).sum())
        fixed = max(1, used // 4)
        passed = fixed + (places - fixed + offset_by * (used - fixed)) % max(1, amount - fixed)
        return jnp.zeros((amount,), jnp.int32).at[order[jnp.where(places < fixed, places, passed)]].set(jnp.asarray(sizes, jnp.int32))

    sizes = jnp.where(number % 4 == 0, named(crowded, number // 4), named(common, number - number // 4 - 1))
    mixed = jax.random.permutation(jax.random.fold_in(own, 3), amount)
    giver, taker = mixed[0:amount // 2 * 2:2], mixed[1:amount // 2 * 2:2]
    margin = jnp.minimum(sizes[giver] - 1, limit - sizes[taker]) // 2
    margin = jnp.where((giver == order[0]) | (taker == order[0]) | (sizes[taker] == 0), 0, jnp.maximum(margin, 0))
    passed = jax.random.randint(jax.random.fold_in(own, 4), (amount // 2,), 0, 1 << 20) % (margin + 1)
    sizes = sizes.at[giver].add(-passed).at[taker].add(passed)
    labels = jnp.searchsorted(jnp.cumsum(sizes), jnp.arange(rows * top), side="right").astype(jnp.int32)
    table = labels.reshape(top, rows).T
    table = table[jax.random.permutation(jax.random.fold_in(own, 1), rows)]
    offset_by = jax.random.randint(jax.random.fold_in(own, 2), (rows, 1), 0, top)
    return jnp.take_along_axis(table, (jnp.arange(top)[None, :] + offset_by) % top, axis=1)


def shares(amount, total, limit, skew, full):
    weights = [(1 << 20) // math.isqrt(standing ** skew) + 1 for standing in range(1, amount + 1)]
    largest = limit if full else min(limit, max(-(-total // amount), total * weights[0] // sum(weights)))
    least = 1 if total - largest >= amount - 1 else 0
    given, rest = [largest] + [least] * (amount - 1), total - largest - least * (amount - 1)
    while rest > 0:
        movable = [i for i in range(1, amount) if given[i] < largest] or [i for i in range(1, amount) if given[i] < limit]
        pool, left = sum([weights[i] for i in movable]), rest
        for i in movable:
            addition = min(limit - given[i], max(1, left * weights[i] // pool), rest)
            given[i] = given[i] + addition
            rest = rest - addition
    return np.array(given)


def normal_values(key, extent, scale, reach, pieces=(), held_as=jnp.bfloat16):
    entries = scale * jax.random.normal(key, extent, jnp.float32)
    if pieces:
        entries = entries * steps_of(key, extent, pieces, -0.22, 0.18)
    return jnp.clip(entries, -reach, reach).astype(held_as)


def setup_inputs(seed: int = 0) -> dict:
    splits = jax.random.split(jax.random.key(seed), 12)
    current = normal_values(splits[0], (K, ROWS), 1.0, 6.0, ((1, 32),), jnp.float32)
    prior = draw_prior(jax.random.fold_in(splits[11], 71), 0)
    block_values = normal_values(splits[2], (P_SIZE * RB, NB, BS * BS), (BS * NB) ** -0.5, 0.25, ((0, 16),), jnp.float32)
    block_cols = plant(jax.random.randint(splits[3], (P_SIZE * RB, NB), 0, RB), jax.random.fold_in(splits[3], 1), 0, RB - 1).astype(jnp.int32)
    face_match = jax.vmap(lambda own: jax.random.permutation(own, FACE))(jax.random.split(splits[4], P_SIZE * ROUNDS)).reshape((P_SIZE, ROUNDS, FACE)).astype(jnp.int32)
    face_weight = normal_values(splits[5], (P_SIZE, ROUNDS, FACE), 0.5, 3.0, ((0, 16),), jnp.float32)
    fluid_diag = jnp.clip(2.0 + 2.0 * jax.random.uniform(splits[6], (P_SIZE * R,), jnp.float32) ** steps_of(splits[6], (P_SIZE * R,), ((0, 16),), -0.2, 0.2), 2.0, 4.0)
    wet_source = plant(jax.random.randint(splits[7], (P_SIZE * WS,), 0, R), jax.random.fold_in(splits[7], 1), 0, R - 1).astype(jnp.int32)
    wet_dest_keys = jax.random.split(jax.random.fold_in(splits[8], 1), (P_SIZE * WS) // WS)
    wet_dest_turns = jax.random.permutation(jax.random.fold_in(splits[8], 3), (P_SIZE * WS) // WS)
    wet_dest = jax.vmap(lambda own, number: shared_out(jax.random.fold_in(splits[8], 2), own, number, WS, P_SIZE, 1, CAP, 2))(wet_dest_keys, wet_dest_turns).reshape((P_SIZE * WS, 1))
    wet_target = plant(jax.random.randint(splits[9], (P_SIZE * WS,), 0, R), jax.random.fold_in(splits[9], 1), 0, R - 1).astype(jnp.int32)
    wet_weight = normal_values(splits[10], (P_SIZE * WS,), 1.0, 5.0, ((0, 16),), jnp.float32)
    return {"current": current, "prior": prior, "block_values": block_values, "block_cols": block_cols, "face_match": face_match, "face_weight": face_weight, "fluid_diag": fluid_diag, "wet_source": wet_source, "wet_dest": wet_dest, "wet_target": wet_target, "wet_weight": wet_weight}


def reference(current, prior, block_values, block_cols, face_match, face_weight, fluid_diag, wet_source, wet_dest, wet_target, wet_weight):
    highest = lax.Precision.HIGHEST
    subdomains = N_GRP * N_DEV
    local_rows = BS * RB
    half_rows = subdomains * local_rows
    structure = current[:, :half_rows].reshape(K, subdomains, local_rows)
    fluid_half = current[:, half_rows:]
    values = block_values.reshape(subdomains, RB, NB, BS, BS)
    columns = block_cols.reshape(subdomains, RB, NB)

    def apply_one(packed):
        block_vals, block_idx, local_vec = packed
        picked = local_vec.reshape(K, RB, BS)[:, block_idx, :]
        return jnp.einsum('kibc,ibrc->kir', picked, block_vals, precision=highest).reshape(K, local_rows)
    shell = lax.map(apply_one, (values, columns, jnp.moveaxis(structure, 1, 0)))
    shell = jnp.moveaxis(shell, 0, 1)
    flips = [1, 2, N_DEV, 2 * N_DEV]
    owners = jnp.arange(subdomains, dtype=jnp.int32)
    for sweep in range(ROUNDS):
        partner = owners ^ flips[sweep]
        faces = structure[:, :, sweep * FACE:(sweep + 1) * FACE][:, partner, :]
        matched = jnp.take_along_axis(faces, face_match[None, :, sweep, :], axis=2)
        shell = shell.at[:, :, sweep * FACE:(sweep + 1) * FACE].add(face_weight[None, :, sweep, :] * matched)
    zero_col = jnp.zeros((K, 1), jnp.float32)
    before = jnp.concatenate([zero_col, fluid_half[:, :-1]], axis=1)
    after = jnp.concatenate([fluid_half[:, 1:], zero_col], axis=1)
    fluid_out = fluid_diag[None, :] * fluid_half - before - after
    couple_owner = jnp.arange(subdomains * WS, dtype=jnp.int32) // WS
    source_cols = couple_owner * local_rows + wet_source
    target_cols = wet_dest[:, 0] * local_rows + wet_target
    moved = wet_weight[None, :] * structure.reshape(K, half_rows)[:, source_cols]
    fluid_flat = fluid_out.at[:, target_cols].add(moved)
    image = jnp.concatenate([shell.reshape(K, half_rows), fluid_flat], axis=1)
    h_first = jnp.einsum('jkr,lr->jkl', prior, image, precision=highest)
    w_one = image - jnp.einsum('jkl,jkr->lr', h_first, prior, precision=highest)
    h_second = jnp.einsum('jkr,lr->jkl', prior, w_one, precision=highest)
    w_two = w_one - jnp.einsum('jkl,jkr->lr', h_second, prior, precision=highest)
    gram = jnp.dot(w_two, w_two.T, precision=highest) / ROWS
    factor = jnp.linalg.cholesky(gram)
    next_block = lax.linalg.triangular_solve(factor, w_two, left_side=True, lower=True)
    return (next_block, h_first + h_second, factor.T)
```

```python
import functools

import jax
import jax.numpy as jnp
from jax import lax
from jax.experimental import pallas as pl
from jax.experimental.pallas import tpu as pltpu
from jax.sharding import PartitionSpec as P

BS = 96
NB = 6
ROUNDS = 4
LANES = 128
META = 8
F32 = jnp.float32
BF16 = jnp.bfloat16
NT = (((1,), (1,)), ((), ()))
ALL = ("sec", "grp", "dev")


def split2(x):
    hi = x.astype(BF16)
    return hi, (x - hi.astype(F32)).astype(BF16)


def nt(a, b):
    return lax.dot_general(a, b, NT, preferred_element_type=F32)


def lane_gather(x, low):
    return jnp.take_along_axis(x, low, axis=1)


def pack_kernel(subdomains, per, x_ref, src_ref, dest_ref, tgt_ref, w_ref, out_ref, meta_ref):
    width, rows = x_ref.shape
    blocks = src_ref.shape[0]
    slabs = subdomains * per
    dest = dest_ref[...]
    lane = lax.broadcasted_iota(jnp.int32, (LANES, LANES), 1)
    sub = lax.broadcasted_iota(jnp.int32, (LANES, LANES), 0)
    tri = jnp.where(sub < lane, 1.0, 0.0).astype(BF16)
    ones = jnp.ones((LANES, LANES), BF16)
    low_tri = jnp.where(
        lax.broadcasted_iota(jnp.int32, (blocks, blocks), 1)
        < lax.broadcasted_iota(jnp.int32, (blocks, blocks), 0),
        1.0,
        0.0,
    ).astype(BF16)

    def count(q, rank):
        mine = dest == q
        oh = jnp.where(mine, 1.0, 0.0).astype(BF16)
        within = jnp.dot(oh, tri, preferred_element_type=F32)
        totals = jnp.dot(oh, ones, preferred_element_type=F32).astype(BF16)
        offset = jnp.dot(low_tri, totals, preferred_element_type=F32)
        return jnp.where(mine, within + offset, rank)

    rank = lax.fori_loop(0, subdomains, count, jnp.zeros(dest.shape, F32)).astype(jnp.int32)
    slab = dest * per + rank // LANES
    spot = rank % LANES
    src = src_ref[...]
    tgt = tgt_ref[...]
    w = w_ref[...]
    w0 = w.astype(BF16).astype(F32)
    w1 = (w - w0).astype(BF16).astype(F32)
    w2 = w - w0 - w1
    fields = [src // LANES, src % LANES, tgt // LANES, tgt % LANES]
    fields = [f.astype(F32) for f in fields] + [w0, w1, w2]
    acc = jnp.zeros((len(fields) * slabs, LANES), F32)
    slab_row = lax.broadcasted_iota(jnp.int32, (slabs, LANES), 0)
    for i in range(blocks):
        hit = slab_row == slab[i : i + 1, :]
        lhs = jnp.concatenate([jnp.where(hit, f[i : i + 1, :], 0.0) for f in fields], axis=0)
        oh = jnp.where(sub == spot[i : i + 1, :], 1.0, 0.0)
        acc = acc + nt(lhs.astype(BF16), oh.astype(BF16))
    parts = [acc[f * slabs : (f + 1) * slabs] for f in range(len(fields))]
    meta_ref[0] = parts[0]
    meta_ref[1] = parts[1]
    meta_ref[2] = parts[2] * LANES + parts[3]
    meta_ref[3] = parts[4] + parts[5] + parts[6]

    def gather(a, carry):
        row = pl.ds(a, 1)
        high = jnp.broadcast_to(meta_ref[0, row, :].astype(jnp.int32), (width, LANES))
        low = jnp.broadcast_to(meta_ref[1, row, :].astype(jnp.int32), (width, LANES))
        got = jnp.zeros((width, LANES), F32)
        for h in range(rows // LANES):
            piece = lane_gather(x_ref[:, h * LANES : (h + 1) * LANES], low)
            got = jnp.where(high == h, piece, got)
        out_ref[a, :width, :] = got * meta_ref[3, row, :]
        out_ref[a, width:, :] = jnp.broadcast_to(meta_ref[2, row, :], (META, LANES))
        return carry

    lax.fori_loop(0, slabs, gather, 0)


def fluid_kernel(x_ref, diag_ref, left_ref, right_ref, got_ref, out_ref, lhs_ref, acc_ref):
    width, rows = x_ref.shape
    slabs = got_ref.shape[0]
    wide = 2 * LANES
    highs = rows // wide
    group = 4
    acc_ref[...] = jnp.zeros_like(acc_ref)

    def step(g, carry):
        ohs = []
        for s in range(group):
            a = g * group + s
            target = got_ref[a, width : width + 1, :].astype(jnp.int32)
            vals = got_ref[a, :width, :]
            hi = vals.astype(BF16).astype(F32)
            lo = vals - hi
            high = jnp.broadcast_to(target // wide, (width, LANES))
            low = target % wide
            at = s * wide
            for h in range(highs):
                hit = high == h
                lhs_ref[h * width : (h + 1) * width, at : at + LANES] = jnp.where(
                    hit, hi, 0.0
                ).astype(BF16)
                lhs_ref[h * width : (h + 1) * width, at + LANES : at + wide] = jnp.where(
                    hit, lo, 0.0
                ).astype(BF16)
            oh = jnp.where(
                lax.broadcasted_iota(jnp.int32, (wide, LANES), 0) == low, 1.0, 0.0
            ).astype(BF16)
            ohs += [oh, oh]
        acc_ref[...] += nt(lhs_ref[...], jnp.concatenate(ohs, axis=1))
        return carry

    lax.fori_loop(0, slabs // group, step, 0)
    lane = lax.broadcasted_iota(jnp.int32, (width, LANES), 1)
    pieces = rows // LANES
    for t in range(pieces):
        own = x_ref[:, t * LANES : (t + 1) * LANES]
        prev = left_ref[...] if t == 0 else x_ref[:, (t - 1) * LANES : t * LANES]
        nxt = right_ref[...] if t == pieces - 1 else x_ref[:, (t + 1) * LANES : (t + 2) * LANES]
        before = jnp.where(lane == 0, pltpu.roll(prev, 1, 1), pltpu.roll(own, 1, 1))
        after = jnp.where(
            lane == LANES - 1, pltpu.roll(nxt, LANES - 1, 1), pltpu.roll(own, LANES - 1, 1)
        )
        h, side = t // 2, t % 2
        added = acc_ref[h * width : (h + 1) * width, side * LANES : (side + 1) * LANES]
        d = diag_ref[:, t * LANES : (t + 1) * LANES]
        out_ref[:, t * LANES : (t + 1) * LANES] = d * own - before - after + added


def face_kernel(y_ref, faces_ref, match_ref, weight_ref, out_ref):
    width = y_ref.shape[0]
    rounds, face = match_ref.shape
    pieces = face // LANES
    for m in range(rounds):
        for o in range(pieces):
            index = match_ref[m : m + 1, o * LANES : (o + 1) * LANES]
            high = jnp.broadcast_to(index // LANES, (width, LANES))
            low = jnp.broadcast_to(index % LANES, (width, LANES))
            got = jnp.zeros((width, LANES), F32)
            for h in range(pieces):
                piece = lane_gather(faces_ref[m, :, h * LANES : (h + 1) * LANES], low)
                got = jnp.where(high == h, piece, got)
            at = m * face + o * LANES
            w = weight_ref[m : m + 1, o * LANES : (o + 1) * LANES]
            out_ref[:, at : at + LANES] = y_ref[:, at : at + LANES] + w * got
    done = rounds * face
    if done < y_ref.shape[1]:
        out_ref[:, done:] = y_ref[:, done:]


def call(kernel, out_shape, *args, scratch=()):
    return pl.pallas_call(
        kernel,
        out_shape=out_shape,
        in_specs=[pl.BlockSpec(memory_space=pltpu.VMEM)] * len(args),
        out_specs=pl.BlockSpec(memory_space=pltpu.VMEM),
        scratch_shapes=list(scratch),
        compiler_params=pltpu.CompilerParams(vmem_limit_bytes=40 << 20),
    )(*args)


def swapped(block, axis, bit):
    count = lax.axis_size(axis)
    route = []
    for low in range(count):
        high = low | 1 << bit
        if high != low and high < count:
            route += [(low, high), (high, low)]
    return lax.ppermute(block, axis, route)


def shards(
    current, prior, block_values, block_cols, face_match, face_weight,
    fluid_diag, wet_source, wet_dest, wet_target, wet_weight,
):
    high = lax.Precision.HIGH
    width, local_rows = current.shape
    face_rows = face_match.shape[2]
    row_blocks = block_cols.shape[0]
    wet_slots = wet_source.shape[0]
    grp, dev = lax.axis_size("grp"), lax.axis_size("dev")
    subdomains = grp * dev
    total_rows = local_rows * lax.axis_size("sec") * subdomains
    capacity = 2 * wet_slots // subdomains + 8
    per = -(-capacity // LANES)
    slabs = subdomains * per
    is_shell = lax.axis_index("sec") == 0
    flat_prior = prior.reshape(-1, local_rows)
    basis = flat_prior.shape[0]
    cross = lax.psum(
        lax.dot_general(flat_prior, flat_prior, NT, precision=high), ALL
    )
    faces = []
    for sweep in range(ROUNDS):
        face_now = current[:, sweep * face_rows : (sweep + 1) * face_rows]
        if sweep < 2:
            faces.append(swapped(face_now, "dev", sweep))
        else:
            faces.append(swapped(face_now, "grp", sweep - 2))
    up = [(i, i + 1) for i in range(subdomains - 1)]
    down = [(j, i) for i, j in up]
    left = lax.ppermute(current[:, -LANES:], ("grp", "dev"), up)
    right = lax.ppermute(current[:, :LANES], ("grp", "dev"), down)
    tiled = (wet_slots // LANES, LANES)

    def pack(x):
        return call(
            functools.partial(pack_kernel, subdomains, per),
            jax.ShapeDtypeStruct((slabs, width + META, LANES), F32),
            x, wet_source.reshape(tiled), wet_dest.reshape(tiled), wet_target.reshape(tiled),
            wet_weight.reshape(tiled), scratch=[pltpu.VMEM((4, slabs, LANES), F32)],
        )

    packed = lax.cond(
        is_shell, pack, lambda x: jnp.zeros((slabs, width + META, LANES), F32), current
    )
    both = jnp.concatenate([jnp.zeros_like(packed), packed], axis=0)
    got = lax.all_to_all(both, ALL, split_axis=0, concat_axis=0, tiled=True)[:slabs]

    def shell_apply(vector):
        picked = vector.reshape(width, row_blocks, BS)[:, block_cols, :]
        matrices = block_values.reshape(row_blocks, NB, BS, BS)
        result = jnp.einsum("kibc,ibrc->kir", picked, matrices, precision=high)
        return call(
            face_kernel, jax.ShapeDtypeStruct((width, local_rows), F32),
            result.reshape(width, local_rows), jnp.stack(faces), face_match[0], face_weight[0],
        )

    def fluid_apply(vector):
        return call(
            fluid_kernel, jax.ShapeDtypeStruct((width, local_rows), F32),
            vector, fluid_diag[None, :], left, right, got,
            scratch=[
                pltpu.VMEM((local_rows // 256 * width, 8 * LANES), BF16),
                pltpu.VMEM((local_rows // 256 * width, 2 * LANES), F32),
            ],
        )

    image = lax.cond(is_shell, shell_apply, fluid_apply, current)
    highest = lax.Precision.HIGHEST
    local = jnp.concatenate(
        [
            lax.dot_general(flat_prior, image, NT, precision=high),
            lax.dot_general(image, image, NT, precision=high),
        ],
        axis=0,
    )
    summed = lax.psum(local, ALL)
    first, square = summed[:basis], summed[basis:]
    coef = 2.0 * first - jnp.dot(cross, first, precision=highest)
    inner = lax.dot_general(coef, first, (((0,), (0,)), ((), ())), precision=highest)
    outer = lax.dot_general(
        coef, jnp.dot(cross, coef, precision=highest), (((0,), (0,)), ((), ())), precision=highest
    )
    gram = (square - inner - inner.T + outer) / total_rows
    factor = jnp.linalg.cholesky(gram)
    inverse = lax.linalg.triangular_solve(
        factor, jnp.eye(width, dtype=F32), left_side=True, lower=True
    )
    mix = -lax.dot_general(inverse, coef, (((1,), (1,)), ((), ())), precision=highest)
    next_block = jnp.dot(inverse, image, precision=high) + jnp.dot(mix, flat_prior, precision=high)
    return (next_block, coef.reshape(prior.shape[0], width, width), factor.T)


def solution(mesh):
    placed = (
        P(None, ALL),
        P(None, None, ALL),
        P(("grp", "dev"), None, None),
        P(("grp", "dev"), None),
        P(("grp", "dev"), None, None),
        P(("grp", "dev"), None, None),
        P(("grp", "dev")),
        P(("grp", "dev")),
        P(("grp", "dev"), None),
        P(("grp", "dev")),
        P(("grp", "dev")),
    )
    return jax.shard_map(
        shards, mesh=mesh, in_specs=placed, out_specs=(P(None, ALL), P(), P()), check_vma=False
    )
```

```python
import functools

import jax
import jax.numpy as jnp
from jax import lax
from jax.experimental import pallas as pl
from jax.experimental.pallas import tpu as pltpu
from jax.sharding import PartitionSpec as P

BS = 96
NB = 6
ROUNDS = 4
LANES = 128
META = 8
F32 = jnp.float32
BF16 = jnp.bfloat16
NT = (((1,), (1,)), ((), ()))
ALL = ("sec", "grp", "dev")


def split2(x):
    hi = x.astype(BF16)
    return hi, (x - hi.astype(F32)).astype(BF16)


def nt(a, b):
    return lax.dot_general(a, b, NT, preferred_element_type=F32)


def lane_gather(x, low):
    return jnp.take_along_axis(x, low, axis=1)


def pack_kernel(subdomains, per, x_ref, src_ref, dest_ref, tgt_ref, w_ref, out_ref, meta_ref):
    width, rows = x_ref.shape
    blocks = src_ref.shape[0]
    slabs = subdomains * per
    dest = dest_ref[...]
    lane = lax.broadcasted_iota(jnp.int32, (LANES, LANES), 1)
    sub = lax.broadcasted_iota(jnp.int32, (LANES, LANES), 0)
    tri = jnp.where(sub < lane, 1.0, 0.0).astype(BF16)
    ones = jnp.ones((LANES, LANES), BF16)
    low_tri = jnp.where(
        lax.broadcasted_iota(jnp.int32, (blocks, blocks), 1)
        < lax.broadcasted_iota(jnp.int32, (blocks, blocks), 0),
        1.0,
        0.0,
    ).astype(BF16)

    def count(q, rank):
        mine = dest == q
        oh = jnp.where(mine, 1.0, 0.0).astype(BF16)
        within = jnp.dot(oh, tri, preferred_element_type=F32)
        totals = jnp.dot(oh, ones, preferred_element_type=F32).astype(BF16)
        offset = jnp.dot(low_tri, totals, preferred_element_type=F32)
        return jnp.where(mine, within + offset, rank)

    rank = lax.fori_loop(0, subdomains, count, jnp.zeros(dest.shape, F32)).astype(jnp.int32)
    slab = dest * per + rank // LANES
    spot = rank % LANES
    src = src_ref[...]
    tgt = tgt_ref[...]
    w = w_ref[...]
    w0 = w.astype(BF16).astype(F32)
    w1 = (w - w0).astype(BF16).astype(F32)
    w2 = w - w0 - w1
    fields = [src // LANES, src % LANES, tgt // LANES, tgt % LANES]
    fields = [f.astype(F32) for f in fields] + [w0, w1, w2]
    acc = jnp.zeros((len(fields) * slabs, LANES), F32)
    slab_row = lax.broadcasted_iota(jnp.int32, (slabs, LANES), 0)
    for i in range(blocks):
        hit = slab_row == slab[i : i + 1, :]
        lhs = jnp.concatenate([jnp.where(hit, f[i : i + 1, :], 0.0) for f in fields], axis=0)
        oh = jnp.where(sub == spot[i : i + 1, :], 1.0, 0.0)
        acc = acc + nt(lhs.astype(BF16), oh.astype(BF16))
    parts = [acc[f * slabs : (f + 1) * slabs] for f in range(len(fields))]
    meta_ref[0] = parts[0]
    meta_ref[1] = parts[1]
    meta_ref[2] = parts[2] * LANES + parts[3]
    meta_ref[3] = parts[4] + parts[5] + parts[6]

    def gather(a, carry):
        row = pl.ds(a, 1)
        high = jnp.broadcast_to(meta_ref[0, row, :].astype(jnp.int32), (width, LANES))
        low = jnp.broadcast_to(meta_ref[1, row, :].astype(jnp.int32), (width, LANES))
        got = jnp.zeros((width, LANES), F32)
        for h in range(rows // LANES):
            piece = lane_gather(x_ref[:, h * LANES : (h + 1) * LANES], low)
            got = jnp.where(high == h, piece, got)
        out_ref[a, :width, :] = got * meta_ref[3, row, :]
        out_ref[a, width:, :] = jnp.broadcast_to(meta_ref[2, row, :], (META, LANES))
        return carry

    lax.fori_loop(0, slabs, gather, 0)


def fluid_kernel(x_ref, diag_ref, left_ref, right_ref, got_ref, out_ref, lhs_ref, acc_ref):
    width, rows = x_ref.shape
    slabs = got_ref.shape[0]
    wide = 2 * LANES
    highs = rows // wide
    group = 4
    acc_ref[...] = jnp.zeros_like(acc_ref)

    def step(g, carry):
        ohs = []
        for s in range(group):
            a = g * group + s
            target = got_ref[a, width : width + 1, :].astype(jnp.int32)
            vals = got_ref[a, :width, :]
            hi = vals.astype(BF16).astype(F32)
            lo = vals - hi
            high = jnp.broadcast_to(target // wide, (width, LANES))
            low = target % wide
            at = s * wide
            for h in range(highs):
                hit = high == h
                lhs_ref[h * width : (h + 1) * width, at : at + LANES] = jnp.where(
                    hit, hi, 0.0
                ).astype(BF16)
                lhs_ref[h * width : (h + 1) * width, at + LANES : at + wide] = jnp.where(
                    hit, lo, 0.0
                ).astype(BF16)
            oh = jnp.where(
                lax.broadcasted_iota(jnp.int32, (wide, LANES), 0) == low, 1.0, 0.0
            ).astype(BF16)
            ohs += [oh, oh]
        acc_ref[...] += nt(lhs_ref[...], jnp.concatenate(ohs, axis=1))
        return carry

    lax.fori_loop(0, slabs // group, step, 0)
    lane = lax.broadcasted_iota(jnp.int32, (width, LANES), 1)
    pieces = rows // LANES
    for t in range(pieces):
        own = x_ref[:, t * LANES : (t + 1) * LANES]
        prev = left_ref[...] if t == 0 else x_ref[:, (t - 1) * LANES : t * LANES]
        nxt = right_ref[...] if t == pieces - 1 else x_ref[:, (t + 1) * LANES : (t + 2) * LANES]
        before = jnp.where(lane == 0, pltpu.roll(prev, 1, 1), pltpu.roll(own, 1, 1))
        after = jnp.where(
            lane == LANES - 1, pltpu.roll(nxt, LANES - 1, 1), pltpu.roll(own, LANES - 1, 1)
        )
        h, side = t // 2, t % 2
        added = acc_ref[h * width : (h + 1) * width, side * LANES : (side + 1) * LANES]
        d = diag_ref[:, t * LANES : (t + 1) * LANES]
        out_ref[:, t * LANES : (t + 1) * LANES] = d * own - before - after + added


def face_kernel(y_ref, faces_ref, match_ref, weight_ref, out_ref):
    width = y_ref.shape[0]
    rounds, face = match_ref.shape
    pieces = face // LANES
    for m in range(rounds):
        for o in range(pieces):
            index = match_ref[m : m + 1, o * LANES : (o + 1) * LANES]
            high = jnp.broadcast_to(index // LANES, (width, LANES))
            low = jnp.broadcast_to(index % LANES, (width, LANES))
            got = jnp.zeros((width, LANES), F32)
            for h in range(pieces):
                piece = lane_gather(faces_ref[m, :, h * LANES : (h + 1) * LANES], low)
                got = jnp.where(high == h, piece, got)
            at = m * face + o * LANES
            w = weight_ref[m : m + 1, o * LANES : (o + 1) * LANES]
            out_ref[:, at : at + LANES] = y_ref[:, at : at + LANES] + w * got
    done = rounds * face
    if done < y_ref.shape[1]:
        out_ref[:, done:] = y_ref[:, done:]


MESH = pl.DeviceIdType.MESH


def place(index):
    dev = lax.axis_size("dev")
    grp = lax.axis_size("grp")
    return (index // (grp * dev), index // dev % grp, index % dev)


def own_index():
    grp, dev = lax.axis_size("grp"), lax.axis_size("dev")
    return (lax.axis_index("sec") * grp + lax.axis_index("grp")) * dev + lax.axis_index("dev")


def everyone(me, n, body):
    def step(s, carry):
        body(lax.rem(me + s, n))
        return carry

    lax.fori_loop(1, n, step, 0)


def announce(me, n):
    barrier = pltpu.get_barrier_semaphore()
    everyone(
        me, n,
        lambda d: pl.semaphore_signal(barrier, inc=1, device_id=place(d), device_id_type=MESH),
    )
    return barrier


def remote(src, dst, send, recv, device):
    return pltpu.make_async_remote_copy(
        src_ref=src, dst_ref=dst, send_sem=send, recv_sem=recv, device_id=device,
        device_id_type=MESH,
    )


class Summing:
    def __init__(self, me, n, stage, slots, total, sems):
        self.me, self.n = me, n
        self.stage, self.slots, self.total, self.sems = stage, slots, total, sems

    def piece(self, to, at):
        return remote(
            self.stage.at[to], self.slots.at[at], self.sems.at[0, to], self.sems.at[1, at],
            place(to),
        )

    def whole(self, to, at):
        return remote(
            self.total.at[at], self.total.at[at], self.sems.at[2, to], self.sems.at[3, at],
            place(to),
        )

    def scatter(self):
        everyone(self.me, self.n, lambda d: self.piece(d, self.me).start())

    def gather(self):
        me = self.me
        everyone(me, self.n, lambda d: self.piece(d, d).wait_recv())
        self.slots[me] = self.stage[me]
        self.total[me] = jnp.sum(self.slots[...], axis=0)
        everyone(me, self.n, lambda d: self.whole(d, me).start())

    def finish(self):
        everyone(self.me, self.n, lambda d: self.whole(d, d).wait_recv())
        everyone(self.me, self.n, lambda d: self.piece(d, d).wait_send())
        everyone(self.me, self.n, lambda d: self.whole(d, self.me).wait_send())


def exchange_kernel(
    subdomains, per, face, x_ref, pack_ref, prior_ref, cross_ref, faces_ref, edge_ref, got_ref,
    stage, slots, total, sems, face_sems, edge_sems, wet_sems,
):
    n = 2 * subdomains
    me = own_index()
    sec, g, d = lax.axis_index("sec"), lax.axis_index("grp"), lax.axis_index("dev")
    mine = lax.rem(me, subdomains)
    rows = x_ref.shape[1]
    partners = [
        (0, g, d + 1 - 2 * lax.rem(d, 2)),
        (0, g, d + 2 - 4 * lax.rem(d // 2, 2)),
        (0, g + 1 - 2 * lax.rem(g, 2), d),
        (0, g + 2 - 4 * lax.rem(g // 2, 2), d),
    ]

    def face_copy(m):
        return remote(
            x_ref.at[:, pl.ds(m * face, face)], faces_ref.at[m], face_sems.at[0, m],
            face_sems.at[1, m], partners[m],
        )

    def edge_copy(side):
        to = subdomains + lax.rem(mine + (1 if side == 0 else subdomains - 1), subdomains)
        at = rows - LANES if side == 0 else 0
        return remote(
            x_ref.at[:, pl.ds(at, LANES)], edge_ref.at[side], edge_sems.at[0, side],
            edge_sems.at[1, side], place(to),
        )

    def wet_copy(to, at):
        return remote(
            pack_ref.at[pl.ds(to * per, per)], got_ref.at[pl.ds(at * per, per)],
            wet_sems.at[0, to], wet_sems.at[1, at], place(subdomains + to),
        )

    def each(body):
        def step(s, carry):
            body(lax.rem(mine + s, subdomains))
            return carry

        lax.fori_loop(0, subdomains, step, 0)

    pl.semaphore_wait(announce(me, n), n - 1)

    @pl.when(sec == 0)
    def _():
        for m in range(ROUNDS):
            face_copy(m).start()
        each(lambda q: wet_copy(q, mine).start())

    @pl.when(sec == 1)
    def _():
        edge_copy(0).start()
        edge_copy(1).start()

    basis = prior_ref.shape[0]
    chunk = 1024

    def product(i, carry):
        same, mixed = carry
        hi, lo = split2(prior_ref[:, pl.ds(pl.multiple_of(i * chunk, chunk), chunk)])
        return same + nt(hi, hi), mixed + nt(hi, lo)

    zero = jnp.zeros((basis, basis), F32)
    same, mixed = lax.fori_loop(0, rows // chunk, product, (zero, zero))
    part = same + mixed + mixed.T
    piece = basis // n
    stage[...] = part.reshape(n, piece, basis)
    summing = Summing(me, n, stage, slots, total, sems)
    summing.scatter()
    summing.gather()
    summing.finish()
    cross_ref[...] = total[...].reshape(basis, basis)

    @pl.when(sec == 0)
    def _():
        for m in range(ROUNDS):
            face_copy(m).wait()
        each(lambda q: wet_copy(q, mine).wait_send())

    @pl.when(sec == 1)
    def _():
        edge_copy(0).wait()
        edge_copy(1).wait()
        each(lambda q: wet_copy(q, q).wait_recv())


def finish_kernel(
    subdomains, total_rows, image_ref, prior_ref, cross_ref, next_ref, coef_ref, fac_ref,
    high_ref, low_ref, stage, slots, total, sems,
):
    n = 2 * subdomains
    me = own_index()
    width, rows = image_ref.shape
    basis = prior_ref.shape[0]
    chunk = 1024
    barrier = announce(me, n)

    def product(i, carry):
        head, square = carry
        at = pl.ds(pl.multiple_of(i * chunk, chunk), chunk)
        hi, lo = split2(prior_ref[:, at])
        high_ref[:, at] = hi
        low_ref[:, at] = lo
        ih, il = split2(image_ref[:, at])
        both = nt(jnp.concatenate([ih, il], axis=0), hi)
        head = head + both[:width] + both[width:] + nt(ih, lo)
        mixed = nt(ih, il)
        square = square + nt(ih, ih) + mixed + mixed.T
        return head, square

    head, square = lax.fori_loop(
        0, rows // chunk, product,
        (jnp.zeros((width, basis), F32), jnp.zeros((width, width), F32)),
    )
    part = jnp.concatenate(
        [head, square, jnp.zeros((width, -(basis + width) % LANES), F32)], axis=1
    )
    cuts = n // width
    span = part.shape[1] // cuts
    for i in range(n):
        row, cut = i // cuts, i % cuts
        stage[i] = part[row : row + 1, cut * span : (cut + 1) * span]
    pl.semaphore_wait(barrier, n - 1)
    summing = Summing(me, n, stage, slots, total, sems)
    summing.scatter()
    summing.gather()
    summing.finish()
    lines = [
        jnp.concatenate([total[r * cuts + c] for c in range(cuts)], axis=1) if cuts > 1 else total[r]
        for r in range(width)
    ]
    summed = jnp.concatenate(lines, axis=0)
    first = summed[:, :basis]
    square = summed[:, basis : basis + width]
    cross = cross_ref[...]
    highest = lax.Precision.HIGHEST

    def dot(a, b):
        return jnp.dot(a, b, precision=highest, preferred_element_type=F32)

    def dot_nt(a, b):
        return lax.dot_general(a, b, NT, precision=highest, preferred_element_type=F32)

    coef = 2.0 * first - dot(first, cross)
    gram = (
        square - dot_nt(coef, first) - dot_nt(first, coef) + dot_nt(dot(coef, cross), coef)
    ) * (1.0 / total_rows)
    coef_ref[...] = coef.T
    sub = lax.broadcasted_iota(jnp.int32, (width, 2 * width), 0)
    lane = lax.broadcasted_iota(jnp.int32, (width, 2 * width), 1)
    eye = jnp.where(sub + width == lane, 1.0, 0.0)
    work = jnp.concatenate([gram, jnp.zeros((width, width), F32)], axis=1) + eye
    for j in range(width):
        root = jnp.sqrt(work[j : j + 1, j : j + 1])
        row = work[j : j + 1, :] / root
        column = work[:, j : j + 1] / root
        work = jnp.where(sub == j, row, jnp.where(sub > j, work - column * row, work))
    fac_ref[...] = jnp.where(sub <= lane, work, 0.0)[:, :width]
    inverse = work[:, width:]
    mix = -dot(inverse, coef)
    vh, vl = split2(inverse)
    mh, ml = split2(mix)
    vs = jnp.concatenate([vh, vl], axis=0)
    ms = jnp.concatenate([mh, ml], axis=0)

    def out(i, carry):
        at = pl.ds(pl.multiple_of(i * chunk, chunk), chunk)
        ih, il = split2(image_ref[:, at])
        a = jnp.dot(ms, high_ref[:, at], preferred_element_type=F32)
        a = a + jnp.dot(vs, ih, preferred_element_type=F32)
        c = jnp.dot(mh, low_ref[:, at], preferred_element_type=F32)
        c = c + jnp.dot(vh, il, preferred_element_type=F32)
        next_ref[:, at] = a[:width] + a[width:] + c
        return carry

    lax.fori_loop(0, rows // chunk, out, 0)


def call(kernel, out_shape, *args, scratch=(), ident=None):
    multi = isinstance(out_shape, (list, tuple))
    spec = pl.BlockSpec(memory_space=pltpu.VMEM)
    return pl.pallas_call(
        kernel,
        out_shape=out_shape,
        in_specs=[spec] * len(args),
        out_specs=tuple([spec] * len(out_shape)) if multi else spec,
        scratch_shapes=list(scratch),
        compiler_params=pltpu.CompilerParams(
            vmem_limit_bytes=40 << 20, collective_id=ident, has_side_effects=ident is not None
        ),
    )(*args)


def shards(
    current, prior, block_values, block_cols, face_match, face_weight,
    fluid_diag, wet_source, wet_dest, wet_target, wet_weight,
):
    high = lax.Precision.HIGH
    width, local_rows = current.shape
    face_rows = face_match.shape[2]
    row_blocks = block_cols.shape[0]
    wet_slots = wet_source.shape[0]
    grp, dev = lax.axis_size("grp"), lax.axis_size("dev")
    subdomains = grp * dev
    total_rows = local_rows * lax.axis_size("sec") * subdomains
    capacity = 2 * wet_slots // subdomains + 8
    per = -(-capacity // LANES)
    slabs = subdomains * per
    is_shell = lax.axis_index("sec") == 0
    flat_prior = prior.reshape(-1, local_rows)
    basis = flat_prior.shape[0]
    tiled = (wet_slots // LANES, LANES)

    def pack(x):
        return call(
            functools.partial(pack_kernel, subdomains, per),
            jax.ShapeDtypeStruct((slabs, width + META, LANES), F32),
            x, wet_source.reshape(tiled), wet_dest.reshape(tiled), wet_target.reshape(tiled),
            wet_weight.reshape(tiled), scratch=[pltpu.VMEM((4, slabs, LANES), F32)],
        )

    packed = lax.cond(
        is_shell, pack, lambda x: jnp.zeros((slabs, width + META, LANES), F32), current
    )
    n = 2 * subdomains
    cross, faces, edges, got = call(
        functools.partial(exchange_kernel, subdomains, per, face_rows),
        (
            jax.ShapeDtypeStruct((basis, basis), F32),
            jax.ShapeDtypeStruct((ROUNDS, width, face_rows), F32),
            jax.ShapeDtypeStruct((2, width, LANES), F32),
            jax.ShapeDtypeStruct(packed.shape, F32),
        ),
        current, packed, flat_prior,
        scratch=[
            pltpu.VMEM((n, basis // n, basis), F32),
            pltpu.VMEM((n, basis // n, basis), F32),
            pltpu.VMEM((n, basis // n, basis), F32),
            pltpu.SemaphoreType.DMA((4, n)),
            pltpu.SemaphoreType.DMA((2, ROUNDS)),
            pltpu.SemaphoreType.DMA((2, 2)),
            pltpu.SemaphoreType.DMA((2, subdomains)),
        ],
        ident=0,
    )
    mine = lax.axis_index("grp") * dev + lax.axis_index("dev")
    left = jnp.where(mine == 0, 0.0, edges[0])
    right = jnp.where(mine == subdomains - 1, 0.0, edges[1])

    def shell_apply(vector):
        picked = vector.reshape(width, row_blocks, BS)[:, block_cols, :]
        matrices = block_values.reshape(row_blocks, NB, BS, BS)
        result = jnp.einsum("kibc,ibrc->kir", picked, matrices, precision=high)
        return call(
            face_kernel, jax.ShapeDtypeStruct((width, local_rows), F32),
            result.reshape(width, local_rows), faces, face_match[0], face_weight[0],
        )

    def fluid_apply(vector):
        return call(
            fluid_kernel, jax.ShapeDtypeStruct((width, local_rows), F32),
            vector, fluid_diag[None, :], left, right, got,
            scratch=[
                pltpu.VMEM((local_rows // 256 * width, 8 * LANES), BF16),
                pltpu.VMEM((local_rows // 256 * width, 2 * LANES), F32),
            ],
        )

    image = lax.cond(is_shell, shell_apply, fluid_apply, current)
    lanes = -(-(basis + width) // LANES) * LANES
    cuts = n // width
    piece = pltpu.VMEM((n, 1, lanes // cuts), F32)
    next_block, coef, factor = call(
        functools.partial(finish_kernel, subdomains, total_rows),
        (
            jax.ShapeDtypeStruct((width, local_rows), F32),
            jax.ShapeDtypeStruct((basis, width), F32),
            jax.ShapeDtypeStruct((width, width), F32),
        ),
        image, flat_prior, cross,
        scratch=[
            pltpu.VMEM((basis, local_rows), BF16),
            pltpu.VMEM((basis, local_rows), BF16),
            piece, piece, piece,
            pltpu.SemaphoreType.DMA((4, n)),
        ],
        ident=1,
    )
    return (next_block, coef.reshape(prior.shape[0], width, width), factor)


def solution(mesh):
    placed = (
        P(None, ALL),
        P(None, None, ALL),
        P(("grp", "dev"), None, None),
        P(("grp", "dev"), None),
        P(("grp", "dev"), None, None),
        P(("grp", "dev"), None, None),
        P(("grp", "dev")),
        P(("grp", "dev")),
        P(("grp", "dev"), None),
        P(("grp", "dev")),
        P(("grp", "dev")),
    )
    return jax.shard_map(
        shards, mesh=mesh, in_specs=placed, out_specs=(P(None, ALL), P(), P()), check_vma=False
    )
```

```python
import functools

import jax
import jax.numpy as jnp
from jax import lax
from jax.experimental import pallas as pl
from jax.experimental.pallas import tpu as pltpu
from jax.sharding import PartitionSpec as P

BS = 96
NB = 6
ROUNDS = 4
LANES = 128
META = 8
F32 = jnp.float32
BF16 = jnp.bfloat16
NT = (((1,), (1,)), ((), ()))
ALL = ("sec", "grp", "dev")


def split2(x):
    hi = x.astype(BF16)
    return hi, (x - hi.astype(F32)).astype(BF16)


def nt(a, b):
    return lax.dot_general(a, b, NT, preferred_element_type=F32)


def lane_gather(x, low):
    return jnp.take_along_axis(x, low, axis=1)


def wet_kernel(
    subdomains, per, x_ref, xs_ref, diag_ref, edge_ref, src_ref, dest_ref, tgt_ref, w_ref, out_ref,
    meta_ref, pack_ref, got_ref, lhs_ref, acc_ref, sems,
):
    @pl.when(lax.axis_index("sec") == 1)
    def _():
        wet_body(
            subdomains, per, x_ref, xs_ref, diag_ref, edge_ref, src_ref, dest_ref, tgt_ref, w_ref,
            out_ref, meta_ref, pack_ref, got_ref, lhs_ref, acc_ref, sems,
        )


def wet_body(
    subdomains, per, own_ref, x_ref, diag_ref, edge_ref, src_ref, dest_ref, tgt_ref, w_ref, image_ref,
    meta_ref, pack_ref, got_ref, lhs_ref, acc_ref, sems,
):
    mine = lax.axis_index("grp") * lax.axis_size("dev") + lax.axis_index("dev")
    barrier = pltpu.get_barrier_semaphore()

    def greet(i, carry):
        other = subdomains + lax.rem(mine + i, subdomains)
        pl.semaphore_signal(barrier, inc=1, device_id=place(other), device_id_type=MESH)
        return carry

    lax.fori_loop(1, subdomains, greet, 0)
    width, rows = x_ref.shape
    blocks = src_ref.shape[0]
    slabs = subdomains * per
    dest = dest_ref[...]
    lane = lax.broadcasted_iota(jnp.int32, (LANES, LANES), 1)
    sub = lax.broadcasted_iota(jnp.int32, (LANES, LANES), 0)
    tri = jnp.where(sub < lane, 1.0, 0.0).astype(BF16)
    ones = jnp.ones((LANES, LANES), BF16)
    low_tri = jnp.where(
        lax.broadcasted_iota(jnp.int32, (blocks, blocks), 1)
        < lax.broadcasted_iota(jnp.int32, (blocks, blocks), 0),
        1.0,
        0.0,
    ).astype(BF16)

    def count(q, rank):
        mine = dest == q
        oh = jnp.where(mine, 1.0, 0.0).astype(BF16)
        within = jnp.dot(oh, tri, preferred_element_type=F32)
        totals = jnp.dot(oh, ones, preferred_element_type=F32).astype(BF16)
        offset = jnp.dot(low_tri, totals, preferred_element_type=F32)
        return jnp.where(mine, within + offset, rank)

    rank = lax.fori_loop(0, subdomains, count, jnp.zeros(dest.shape, F32)).astype(jnp.int32)
    slab = dest * per + rank // LANES
    spot = rank % LANES
    src = src_ref[...]
    tgt = tgt_ref[...]
    w = w_ref[...]
    w0 = w.astype(BF16).astype(F32)
    w1 = (w - w0).astype(BF16).astype(F32)
    w2 = w - w0 - w1
    fields = [src // LANES, src % LANES, tgt // LANES, tgt % LANES]
    fields = [f.astype(F32) for f in fields] + [w0, w1, w2]
    acc = jnp.zeros((len(fields) * slabs, LANES), F32)
    slab_row = lax.broadcasted_iota(jnp.int32, (slabs, LANES), 0)
    for i in range(blocks):
        hit = slab_row == slab[i : i + 1, :]
        lhs = jnp.concatenate([jnp.where(hit, f[i : i + 1, :], 0.0) for f in fields], axis=0)
        oh = jnp.where(sub == spot[i : i + 1, :], 1.0, 0.0)
        acc = acc + nt(lhs.astype(BF16), oh.astype(BF16))
    parts = [acc[f * slabs : (f + 1) * slabs] for f in range(len(fields))]
    meta_ref[0] = parts[0]
    meta_ref[1] = parts[1]
    meta_ref[2] = parts[2] * LANES + parts[3]
    meta_ref[3] = parts[4] + parts[5] + parts[6]

    def gather(a, ref, to):
        row = pl.ds(a, 1)
        high = jnp.broadcast_to(meta_ref[0, row, :].astype(jnp.int32), (width, LANES))
        low = jnp.broadcast_to(meta_ref[1, row, :].astype(jnp.int32), (width, LANES))
        got = jnp.zeros((width, LANES), F32)
        for h in range(rows // LANES):
            piece = lane_gather(x_ref[:, h * LANES : (h + 1) * LANES], low)
            got = jnp.where(high == h, piece, got)
        ref[to, :width, :] = got * meta_ref[3, row, :]
        ref[to, width:, :] = jnp.broadcast_to(meta_ref[2, row, :], (META, LANES))

    def copy(to, at):
        return remote(
            pack_ref.at[pl.ds(to * per, per)], got_ref.at[pl.ds(at * per, per)], sems.at[0, to],
            sems.at[1, at], place(subdomains + to),
        )

    pl.semaphore_wait(barrier, subdomains - 1)

    def send(s, carry):
        q = lax.rem(mine + s, subdomains)

        def one(p, inner):
            gather(q * per + p, pack_ref, q * per + p)
            return inner

        lax.fori_loop(0, per, one, 0)
        copy(q, mine).start()
        return carry

    lax.fori_loop(1, subdomains, send, 0)

    def keep(p, inner):
        gather(mine * per + p, got_ref, mine * per + p)
        return inner

    lax.fori_loop(0, per, keep, 0)
    wide = 2 * LANES
    highs = rows // wide
    acc_ref[...] = jnp.zeros_like(acc_ref)

    def add(q):
        ohs = []
        for s in range(per):
            a = q * per + s
            target = got_ref[a, width : width + 1, :].astype(jnp.int32)
            vals = got_ref[a, :width, :]
            hi = vals.astype(BF16).astype(F32)
            lo = vals - hi
            high = jnp.broadcast_to(target // wide, (width, LANES))
            low = target % wide
            at = s * wide
            for h in range(highs):
                hit = high == h
                band = slice(h * width, (h + 1) * width)
                lhs_ref[band, at : at + LANES] = jnp.where(hit, hi, 0.0).astype(BF16)
                lhs_ref[band, at + LANES : at + wide] = jnp.where(hit, lo, 0.0).astype(BF16)
            oh = jnp.where(
                lax.broadcasted_iota(jnp.int32, (wide, LANES), 0) == low, 1.0, 0.0
            ).astype(BF16)
            ohs += [oh, oh]
        acc_ref[...] += nt(lhs_ref[...], jnp.concatenate(ohs, axis=1))

    add(mine)

    def take(s, carry):
        q = lax.rem(mine + subdomains - s, subdomains)
        copy(q, q).wait_recv()
        add(q)
        return carry

    lax.fori_loop(1, subdomains, take, 0)

    def drain(s, carry):
        copy(lax.rem(mine + s, subdomains), mine).wait_send()
        return carry

    lax.fori_loop(1, subdomains, drain, 0)
    edges = [
        jnp.where(mine == 0, 0.0, edge_ref[0]),
        jnp.where(mine == subdomains - 1, 0.0, edge_ref[1]),
    ]
    lane = lax.broadcasted_iota(jnp.int32, (width, LANES), 1)
    pieces = rows // LANES
    for t in range(pieces):
        own = own_ref[:, t * LANES : (t + 1) * LANES]
        prev = edges[0] if t == 0 else own_ref[:, (t - 1) * LANES : t * LANES]
        nxt = edges[1] if t == pieces - 1 else own_ref[:, (t + 1) * LANES : (t + 2) * LANES]
        before = jnp.where(lane == 0, pltpu.roll(prev, 1, 1), pltpu.roll(own, 1, 1))
        after = jnp.where(
            lane == LANES - 1, pltpu.roll(nxt, LANES - 1, 1), pltpu.roll(own, LANES - 1, 1)
        )
        h, side = t // 2, t % 2
        added = acc_ref[h * width : (h + 1) * width, side * LANES : (side + 1) * LANES]
        d = diag_ref[:, t * LANES : (t + 1) * LANES]
        image_ref[:, t * LANES : (t + 1) * LANES] = d * own - before - after + added


def face_kernel(y_ref, faces_ref, match_ref, weight_ref, out_ref):
    width = y_ref.shape[0]
    rounds, face = match_ref.shape
    pieces = face // LANES
    for m in range(rounds):
        for o in range(pieces):
            index = match_ref[m : m + 1, o * LANES : (o + 1) * LANES]
            high = jnp.broadcast_to(index // LANES, (width, LANES))
            low = jnp.broadcast_to(index % LANES, (width, LANES))
            got = jnp.zeros((width, LANES), F32)
            for h in range(pieces):
                piece = lane_gather(faces_ref[m, :, h * LANES : (h + 1) * LANES], low)
                got = jnp.where(high == h, piece, got)
            at = m * face + o * LANES
            w = weight_ref[m : m + 1, o * LANES : (o + 1) * LANES]
            out_ref[:, at : at + LANES] = y_ref[:, at : at + LANES] + w * got
    done = rounds * face
    if done < y_ref.shape[1]:
        out_ref[:, done:] = y_ref[:, done:]


MESH = pl.DeviceIdType.MESH


def place(index):
    dev = lax.axis_size("dev")
    grp = lax.axis_size("grp")
    return (index // (grp * dev), index // dev % grp, index % dev)


def own_index():
    grp, dev = lax.axis_size("grp"), lax.axis_size("dev")
    return (lax.axis_index("sec") * grp + lax.axis_index("grp")) * dev + lax.axis_index("dev")


def everyone(me, n, body):
    def step(s, carry):
        body(lax.rem(me + s, n))
        return carry

    lax.fori_loop(1, n, step, 0)


def announce(me, n):
    barrier = pltpu.get_barrier_semaphore()
    everyone(
        me, n,
        lambda d: pl.semaphore_signal(barrier, inc=1, device_id=place(d), device_id_type=MESH),
    )
    return barrier


def remote(src, dst, send, recv, device):
    return pltpu.make_async_remote_copy(
        src_ref=src, dst_ref=dst, send_sem=send, recv_sem=recv, device_id=device,
        device_id_type=MESH,
    )


class Summing:
    def __init__(self, me, n, stage, slots, total, sems):
        self.me, self.n = me, n
        self.stage, self.slots, self.total, self.sems = stage, slots, total, sems

    def piece(self, to, at):
        return remote(
            self.stage.at[to], self.slots.at[at], self.sems.at[0, to], self.sems.at[1, at],
            place(to),
        )

    def whole(self, to, at):
        return remote(
            self.total.at[at], self.total.at[at], self.sems.at[2, to], self.sems.at[3, at],
            place(to),
        )

    def scatter(self):
        everyone(self.me, self.n, lambda d: self.piece(d, self.me).start())

    def gather(self):
        me = self.me
        everyone(me, self.n, lambda d: self.piece(d, d).wait_recv())
        self.slots[me] = self.stage[me]
        self.total[me] = jnp.sum(self.slots[...], axis=0)
        everyone(me, self.n, lambda d: self.whole(d, me).start())

    def finish(self):
        everyone(self.me, self.n, lambda d: self.whole(d, d).wait_recv())
        everyone(self.me, self.n, lambda d: self.piece(d, d).wait_send())
        everyone(self.me, self.n, lambda d: self.whole(d, self.me).wait_send())


def exchange_kernel(
    subdomains, face, x_ref, prior_ref, cross_ref, faces_ref, edge_ref, xs_ref,
    stage, slots, total, sems, face_sems, edge_sems, twin_sems,
):
    n = 2 * subdomains
    me = own_index()
    sec, g, d = lax.axis_index("sec"), lax.axis_index("grp"), lax.axis_index("dev")
    mine = lax.rem(me, subdomains)
    rows = x_ref.shape[1]
    partners = [
        (0, g, d + 1 - 2 * lax.rem(d, 2)),
        (0, g, d + 2 - 4 * lax.rem(d // 2, 2)),
        (0, g + 1 - 2 * lax.rem(g, 2), d),
        (0, g + 2 - 4 * lax.rem(g // 2, 2), d),
    ]

    def face_copy(m):
        return remote(
            x_ref.at[:, pl.ds(m * face, face)], faces_ref.at[m], face_sems.at[0, m],
            face_sems.at[1, m], partners[m],
        )

    def edge_copy(side):
        to = subdomains + lax.rem(mine + (1 if side == 0 else subdomains - 1), subdomains)
        at = rows - LANES if side == 0 else 0
        return remote(
            x_ref.at[:, pl.ds(at, LANES)], edge_ref.at[side], edge_sems.at[0, side],
            edge_sems.at[1, side], place(to),
        )

    def twin_copy():
        return remote(x_ref, xs_ref, twin_sems.at[0], twin_sems.at[1], (1, g, d))

    pl.semaphore_wait(announce(me, n), n - 1)

    @pl.when(sec == 0)
    def _():
        twin_copy().start()
        for m in range(ROUNDS):
            face_copy(m).start()

    @pl.when(sec == 1)
    def _():
        edge_copy(0).start()
        edge_copy(1).start()

    basis = prior_ref.shape[0]
    chunk = 1024

    def product(i, carry):
        same, mixed = carry
        hi, lo = split2(prior_ref[:, pl.ds(pl.multiple_of(i * chunk, chunk), chunk)])
        return same + nt(hi, hi), mixed + nt(hi, lo)

    zero = jnp.zeros((basis, basis), F32)
    same, mixed = lax.fori_loop(0, rows // chunk, product, (zero, zero))
    part = same + mixed + mixed.T
    piece = basis // n
    stage[...] = part.reshape(n, piece, basis)
    summing = Summing(me, n, stage, slots, total, sems)
    summing.scatter()
    summing.gather()
    summing.finish()
    cross_ref[...] = total[...].reshape(basis, basis)

    @pl.when(sec == 0)
    def _():
        for m in range(ROUNDS):
            face_copy(m).wait()
        twin_copy().wait_send()

    @pl.when(sec == 1)
    def _():
        edge_copy(0).wait()
        edge_copy(1).wait()
        twin_copy().wait_recv()


def finish_kernel(
    subdomains, total_rows, image_ref, prior_ref, cross_ref, next_ref, coef_ref, fac_ref,
    high_ref, low_ref, stage, slots, total, sems,
):
    n = 2 * subdomains
    me = own_index()
    width, rows = image_ref.shape
    basis = prior_ref.shape[0]
    chunk = 1024
    barrier = announce(me, n)

    def product(i, carry):
        head, square = carry
        at = pl.ds(pl.multiple_of(i * chunk, chunk), chunk)
        hi, lo = split2(prior_ref[:, at])
        high_ref[:, at] = hi
        low_ref[:, at] = lo
        ih, il = split2(image_ref[:, at])
        both = nt(jnp.concatenate([ih, il], axis=0), hi)
        head = head + both[:width] + both[width:] + nt(ih, lo)
        mixed = nt(ih, il)
        square = square + nt(ih, ih) + mixed + mixed.T
        return head, square

    head, square = lax.fori_loop(
        0, rows // chunk, product,
        (jnp.zeros((width, basis), F32), jnp.zeros((width, width), F32)),
    )
    part = jnp.concatenate(
        [head, square, jnp.zeros((width, -(basis + width) % LANES), F32)], axis=1
    )
    cuts = n // width
    span = part.shape[1] // cuts
    for i in range(n):
        row, cut = i // cuts, i % cuts
        stage[i] = part[row : row + 1, cut * span : (cut + 1) * span]
    pl.semaphore_wait(barrier, n - 1)
    summing = Summing(me, n, stage, slots, total, sems)
    summing.scatter()
    summing.gather()
    summing.finish()
    lines = [
        jnp.concatenate([total[r * cuts + c] for c in range(cuts)], axis=1) if cuts > 1 else total[r]
        for r in range(width)
    ]
    summed = jnp.concatenate(lines, axis=0)
    first = summed[:, :basis]
    square = summed[:, basis : basis + width]
    cross = cross_ref[...]
    highest = lax.Precision.HIGHEST

    def dot(a, b):
        return jnp.dot(a, b, precision=highest, preferred_element_type=F32)

    def dot_nt(a, b):
        return lax.dot_general(a, b, NT, precision=highest, preferred_element_type=F32)

    coef = 2.0 * first - dot(first, cross)
    gram = (
        square - dot_nt(coef, first) - dot_nt(first, coef) + dot_nt(dot(coef, cross), coef)
    ) * (1.0 / total_rows)
    coef_ref[...] = coef.T
    sub = lax.broadcasted_iota(jnp.int32, (width, 2 * width), 0)
    lane = lax.broadcasted_iota(jnp.int32, (width, 2 * width), 1)
    eye = jnp.where(sub + width == lane, 1.0, 0.0)
    work = jnp.concatenate([gram, jnp.zeros((width, width), F32)], axis=1) + eye
    for j in range(width):
        root = jnp.sqrt(work[j : j + 1, j : j + 1])
        row = work[j : j + 1, :] / root
        column = work[:, j : j + 1] / root
        work = jnp.where(sub == j, row, jnp.where(sub > j, work - column * row, work))
    fac_ref[...] = jnp.where(sub <= lane, work, 0.0)[:, :width]
    inverse = work[:, width:]
    mix = -dot(inverse, coef)
    vh, vl = split2(inverse)
    mh, ml = split2(mix)
    vs = jnp.concatenate([vh, vl], axis=0)
    ms = jnp.concatenate([mh, ml], axis=0)

    def out(i, carry):
        at = pl.ds(pl.multiple_of(i * chunk, chunk), chunk)
        ih, il = split2(image_ref[:, at])
        a = jnp.dot(ms, high_ref[:, at], preferred_element_type=F32)
        a = a + jnp.dot(vs, ih, preferred_element_type=F32)
        c = jnp.dot(mh, low_ref[:, at], preferred_element_type=F32)
        c = c + jnp.dot(vh, il, preferred_element_type=F32)
        next_ref[:, at] = a[:width] + a[width:] + c
        return carry

    lax.fori_loop(0, rows // chunk, out, 0)


def call(kernel, out_shape, *args, scratch=(), ident=None):
    multi = isinstance(out_shape, (list, tuple))
    spec = pl.BlockSpec(memory_space=pltpu.VMEM)
    return pl.pallas_call(
        kernel,
        out_shape=out_shape,
        in_specs=[spec] * len(args),
        out_specs=tuple([spec] * len(out_shape)) if multi else spec,
        scratch_shapes=list(scratch),
        compiler_params=pltpu.CompilerParams(
            vmem_limit_bytes=40 << 20, collective_id=ident, has_side_effects=ident is not None
        ),
    )(*args)


def shards(
    current, prior, block_values, block_cols, face_match, face_weight,
    fluid_diag, wet_source, wet_dest, wet_target, wet_weight,
):
    high = lax.Precision.HIGH
    width, local_rows = current.shape
    face_rows = face_match.shape[2]
    row_blocks = block_cols.shape[0]
    wet_slots = wet_source.shape[0]
    grp, dev = lax.axis_size("grp"), lax.axis_size("dev")
    subdomains = grp * dev
    total_rows = local_rows * lax.axis_size("sec") * subdomains
    capacity = 2 * wet_slots // subdomains + 8
    per = -(-capacity // LANES)
    slabs = subdomains * per
    is_shell = lax.axis_index("sec") == 0
    flat_prior = prior.reshape(-1, local_rows)
    basis = flat_prior.shape[0]
    n = 2 * subdomains
    cross, faces, edges, twin = call(
        functools.partial(exchange_kernel, subdomains, face_rows),
        (
            jax.ShapeDtypeStruct((basis, basis), F32),
            jax.ShapeDtypeStruct((ROUNDS, width, face_rows), F32),
            jax.ShapeDtypeStruct((2, width, LANES), F32),
            jax.ShapeDtypeStruct(current.shape, F32),
        ),
        current, flat_prior,
        scratch=[
            pltpu.VMEM((n, basis // n, basis), F32),
            pltpu.VMEM((n, basis // n, basis), F32),
            pltpu.VMEM((n, basis // n, basis), F32),
            pltpu.SemaphoreType.DMA((4, n)),
            pltpu.SemaphoreType.DMA((2, ROUNDS)),
            pltpu.SemaphoreType.DMA((2, 2)),
            pltpu.SemaphoreType.DMA((2,)),
        ],
        ident=0,
    )
    tiled = (wet_slots // LANES, LANES)
    bands = local_rows // (2 * LANES) * width
    slab = pltpu.VMEM((slabs, width + META, LANES), F32)
    fluid = call(
        functools.partial(wet_kernel, subdomains, per),
        jax.ShapeDtypeStruct((width, local_rows), F32),
        current, twin, fluid_diag[None, :], edges, wet_source.reshape(tiled),
        wet_dest.reshape(tiled), wet_target.reshape(tiled), wet_weight.reshape(tiled),
        scratch=[
            pltpu.VMEM((4, slabs, LANES), F32),
            slab,
            slab,
            pltpu.VMEM((bands, 2 * per * LANES), BF16),
            pltpu.VMEM((bands, 2 * LANES), F32),
            pltpu.SemaphoreType.DMA((2, subdomains)),
        ],
        ident=2,
    )

    def shell_apply(vector):
        picked = vector.reshape(width, row_blocks, BS)[:, block_cols, :]
        matrices = block_values.reshape(row_blocks, NB, BS, BS)
        result = jnp.einsum("kibc,ibrc->kir", picked, matrices, precision=high)
        return call(
            face_kernel, jax.ShapeDtypeStruct((width, local_rows), F32),
            result.reshape(width, local_rows), faces, face_match[0], face_weight[0],
        )

    image = lax.cond(is_shell, shell_apply, lambda x: fluid, current)
    lanes = -(-(basis + width) // LANES) * LANES
    cuts = n // width
    piece = pltpu.VMEM((n, 1, lanes // cuts), F32)
    next_block, coef, factor = call(
        functools.partial(finish_kernel, subdomains, total_rows),
        (
            jax.ShapeDtypeStruct((width, local_rows), F32),
            jax.ShapeDtypeStruct((basis, width), F32),
            jax.ShapeDtypeStruct((width, width), F32),
        ),
        image, flat_prior, cross,
        scratch=[
            pltpu.VMEM((basis, local_rows), BF16),
            pltpu.VMEM((basis, local_rows), BF16),
            piece, piece, piece,
            pltpu.SemaphoreType.DMA((4, n)),
        ],
        ident=1,
    )
    return (next_block, coef.reshape(prior.shape[0], width, width), factor)


def solution(mesh):
    placed = (
        P(None, ALL),
        P(None, None, ALL),
        P(("grp", "dev"), None, None),
        P(("grp", "dev"), None),
        P(("grp", "dev"), None, None),
        P(("grp", "dev"), None, None),
        P(("grp", "dev")),
        P(("grp", "dev")),
        P(("grp", "dev"), None),
        P(("grp", "dev")),
        P(("grp", "dev")),
    )
    return jax.shard_map(
        shards, mesh=mesh, in_specs=placed, out_specs=(P(None, ALL), P(), P()), check_vma=False
    )
```

```python
import functools

import jax
import jax.numpy as jnp
from jax import lax
from jax.experimental import pallas as pl
from jax.experimental.pallas import tpu as pltpu
from jax.sharding import PartitionSpec as P

BS = 96
NB = 6
ROUNDS = 4
LANES = 128
META = 8
F32 = jnp.float32
BF16 = jnp.bfloat16
NT = (((1,), (1,)), ((), ()))
ALL = ("sec", "grp", "dev")


def split2(x):
    hi = x.astype(BF16)
    return hi, (x - hi.astype(F32)).astype(BF16)


def nt(a, b):
    return lax.dot_general(a, b, NT, preferred_element_type=F32)


def lane_gather(x, low):
    return jnp.take_along_axis(x, low, axis=1)


def wet_kernel(
    subdomains, per, x_ref, xs_ref, diag_ref, edge_ref, src_ref, dest_ref, tgt_ref, w_ref, out_ref,
    meta_ref, pack_ref, got_ref, lhs_ref, acc_ref, sems,
):
    @pl.when(lax.axis_index("sec") == 1)
    def _():
        wet_body(
            subdomains, per, x_ref, xs_ref, diag_ref, edge_ref, src_ref, dest_ref, tgt_ref, w_ref,
            out_ref, meta_ref, pack_ref, got_ref, lhs_ref, acc_ref, sems,
        )


def wet_body(
    subdomains, per, own_ref, x_ref, diag_ref, edge_ref, src_ref, dest_ref, tgt_ref, w_ref, image_ref,
    meta_ref, pack_ref, got_ref, lhs_ref, acc_ref, sems,
):
    mine = lax.axis_index("grp") * lax.axis_size("dev") + lax.axis_index("dev")
    barrier = pltpu.get_barrier_semaphore()

    def greet(i, carry):
        other = subdomains + lax.rem(mine + i, subdomains)
        pl.semaphore_signal(barrier, inc=1, device_id=place(other), device_id_type=MESH)
        return carry

    lax.fori_loop(1, subdomains, greet, 0)
    width, rows = x_ref.shape
    blocks = src_ref.shape[0]
    slabs = subdomains * per
    dest = dest_ref[...]
    lane = lax.broadcasted_iota(jnp.int32, (LANES, LANES), 1)
    sub = lax.broadcasted_iota(jnp.int32, (LANES, LANES), 0)
    tri = jnp.where(sub < lane, 1.0, 0.0).astype(BF16)
    ones = jnp.ones((LANES, LANES), BF16)
    low_tri = jnp.where(
        lax.broadcasted_iota(jnp.int32, (blocks, blocks), 1)
        < lax.broadcasted_iota(jnp.int32, (blocks, blocks), 0),
        1.0,
        0.0,
    ).astype(BF16)

    def count(q, rank):
        mine = dest == q
        oh = jnp.where(mine, 1.0, 0.0).astype(BF16)
        within = jnp.dot(oh, tri, preferred_element_type=F32)
        totals = jnp.dot(oh, ones, preferred_element_type=F32).astype(BF16)
        offset = jnp.dot(low_tri, totals, preferred_element_type=F32)
        return jnp.where(mine, within + offset, rank)

    rank = lax.fori_loop(0, subdomains, count, jnp.zeros(dest.shape, F32)).astype(jnp.int32)
    slab = dest * per + rank // LANES
    spot = rank % LANES
    src = src_ref[...]
    tgt = tgt_ref[...]
    w = w_ref[...]
    w0 = w.astype(BF16).astype(F32)
    w1 = (w - w0).astype(BF16).astype(F32)
    w2 = w - w0 - w1
    fields = [src // LANES, src % LANES, tgt // LANES, tgt % LANES]
    fields = [f.astype(F32) for f in fields] + [w0, w1, w2]
    acc = jnp.zeros((len(fields) * slabs, LANES), F32)
    slab_row = lax.broadcasted_iota(jnp.int32, (slabs, LANES), 0)
    for i in range(blocks):
        hit = slab_row == slab[i : i + 1, :]
        lhs = jnp.concatenate([jnp.where(hit, f[i : i + 1, :], 0.0) for f in fields], axis=0)
        oh = jnp.where(sub == spot[i : i + 1, :], 1.0, 0.0)
        acc = acc + nt(lhs.astype(BF16), oh.astype(BF16))
    parts = [acc[f * slabs : (f + 1) * slabs] for f in range(len(fields))]
    meta_ref[0] = parts[0]
    meta_ref[1] = parts[1]
    meta_ref[2] = parts[2] * LANES + parts[3]
    meta_ref[3] = parts[4] + parts[5] + parts[6]

    def gather(a, ref, to):
        row = pl.ds(a, 1)
        high = jnp.broadcast_to(meta_ref[0, row, :].astype(jnp.int32), (width, LANES))
        low = jnp.broadcast_to(meta_ref[1, row, :].astype(jnp.int32), (width, LANES))
        got = jnp.zeros((width, LANES), F32)
        for h in range(rows // LANES):
            piece = lane_gather(x_ref[:, h * LANES : (h + 1) * LANES], low)
            got = jnp.where(high == h, piece, got)
        ref[to, :width, :] = got * meta_ref[3, row, :]
        ref[to, width:, :] = jnp.broadcast_to(meta_ref[2, row, :], (META, LANES))

    def copy(to, at):
        return remote(
            pack_ref.at[pl.ds(to * per, per)], got_ref.at[pl.ds(at * per, per)], sems.at[0, to],
            sems.at[1, at], place(subdomains + to),
        )

    pl.semaphore_wait(barrier, subdomains - 1)

    def send(s, carry):
        q = lax.rem(mine + s, subdomains)

        def one(p, inner):
            gather(q * per + p, pack_ref, q * per + p)
            return inner

        lax.fori_loop(0, per, one, 0)
        copy(q, mine).start()
        return carry

    lax.fori_loop(1, subdomains, send, 0)

    def keep(p, inner):
        gather(mine * per + p, got_ref, mine * per + p)
        return inner

    lax.fori_loop(0, per, keep, 0)
    wide = 2 * LANES
    highs = rows // wide
    acc_ref[...] = jnp.zeros_like(acc_ref)

    def add(q):
        ohs = []
        for s in range(per):
            a = q * per + s
            target = got_ref[a, width : width + 1, :].astype(jnp.int32)
            vals = got_ref[a, :width, :]
            hi = vals.astype(BF16).astype(F32)
            lo = vals - hi
            high = jnp.broadcast_to(target // wide, (width, LANES))
            low = target % wide
            at = s * wide
            for h in range(highs):
                hit = high == h
                band = slice(h * width, (h + 1) * width)
                lhs_ref[band, at : at + LANES] = jnp.where(hit, hi, 0.0).astype(BF16)
                lhs_ref[band, at + LANES : at + wide] = jnp.where(hit, lo, 0.0).astype(BF16)
            oh = jnp.where(
                lax.broadcasted_iota(jnp.int32, (wide, LANES), 0) == low, 1.0, 0.0
            ).astype(BF16)
            ohs += [oh, oh]
        acc_ref[...] += nt(lhs_ref[...], jnp.concatenate(ohs, axis=1))

    add(mine)

    def take(s, carry):
        q = lax.rem(mine + subdomains - s, subdomains)
        copy(q, q).wait_recv()
        add(q)
        return carry

    lax.fori_loop(1, subdomains, take, 0)

    def drain(s, carry):
        copy(lax.rem(mine + s, subdomains), mine).wait_send()
        return carry

    lax.fori_loop(1, subdomains, drain, 0)
    edges = [
        jnp.where(mine == 0, 0.0, edge_ref[0]),
        jnp.where(mine == subdomains - 1, 0.0, edge_ref[1]),
    ]
    lane = lax.broadcasted_iota(jnp.int32, (width, LANES), 1)
    pieces = rows // LANES
    for t in range(pieces):
        own = own_ref[:, t * LANES : (t + 1) * LANES]
        prev = edges[0] if t == 0 else own_ref[:, (t - 1) * LANES : t * LANES]
        nxt = edges[1] if t == pieces - 1 else own_ref[:, (t + 1) * LANES : (t + 2) * LANES]
        before = jnp.where(lane == 0, pltpu.roll(prev, 1, 1), pltpu.roll(own, 1, 1))
        after = jnp.where(
            lane == LANES - 1, pltpu.roll(nxt, LANES - 1, 1), pltpu.roll(own, LANES - 1, 1)
        )
        h, side = t // 2, t % 2
        added = acc_ref[h * width : (h + 1) * width, side * LANES : (side + 1) * LANES]
        d = diag_ref[:, t * LANES : (t + 1) * LANES]
        image_ref[:, t * LANES : (t + 1) * LANES] = d * own - before - after + added


def face_kernel(y_ref, faces_ref, match_ref, weight_ref, out_ref):
    width = y_ref.shape[0]
    rounds, face = match_ref.shape
    pieces = face // LANES
    for m in range(rounds):
        for o in range(pieces):
            index = match_ref[m : m + 1, o * LANES : (o + 1) * LANES]
            high = jnp.broadcast_to(index // LANES, (width, LANES))
            low = jnp.broadcast_to(index % LANES, (width, LANES))
            got = jnp.zeros((width, LANES), F32)
            for h in range(pieces):
                piece = lane_gather(faces_ref[m, :, h * LANES : (h + 1) * LANES], low)
                got = jnp.where(high == h, piece, got)
            at = m * face + o * LANES
            w = weight_ref[m : m + 1, o * LANES : (o + 1) * LANES]
            out_ref[:, at : at + LANES] = y_ref[:, at : at + LANES] + w * got
    done = rounds * face
    if done < y_ref.shape[1]:
        out_ref[:, done:] = y_ref[:, done:]


MESH = pl.DeviceIdType.MESH


def place(index):
    dev = lax.axis_size("dev")
    grp = lax.axis_size("grp")
    return (index // (grp * dev), index // dev % grp, index % dev)


def own_index():
    grp, dev = lax.axis_size("grp"), lax.axis_size("dev")
    return (lax.axis_index("sec") * grp + lax.axis_index("grp")) * dev + lax.axis_index("dev")


def everyone(body):
    counts = [lax.axis_size(axis) for axis in ALL]
    turns = []
    for axis, count in zip(ALL, counts):
        at = lax.axis_index(axis)
        ring = [at]
        for _ in range(1, count):
            following = ring[-1] + 1
            ring.append(jnp.where(following == count, 0, following))
        turns.append(ring)
    for i in range(counts[0]):
        for j in range(counts[1]):
            for k in range(counts[2]):
                if i or j or k:
                    where = (turns[0][i], turns[1][j], turns[2][k])
                    body((where[0] * counts[1] + where[1]) * counts[2] + where[2], where)


def announce():
    barrier = pltpu.get_barrier_semaphore()
    everyone(
        lambda d, where: pl.semaphore_signal(
            barrier, inc=1, device_id=where, device_id_type=MESH
        )
    )
    return barrier


def stream(prior_ref, held, sems, chunk):
    def copy(i):
        at = pl.ds(pl.multiple_of(i * chunk, chunk), chunk)
        return pltpu.make_async_copy(prior_ref.at[:, at], held.at[:, at], sems.at[i])

    return copy


def remote(src, dst, send, recv, device):
    return pltpu.make_async_remote_copy(
        src_ref=src, dst_ref=dst, send_sem=send, recv_sem=recv, device_id=device,
        device_id_type=MESH,
    )


class Summing:
    def __init__(self, me, n, stage, slots, total, sems):
        self.me, self.n = me, n
        self.stage, self.slots, self.total, self.sems = stage, slots, total, sems

    def scatter(self):
        everyone(
            lambda d, where: remote(
                self.stage.at[d], self.slots.at[self.me], self.sems.at[0], self.sems.at[1], where
            ).start()
        )

    def bulk(self, source, target, first):
        rest = pl.ds(0, self.n - 1)
        other = (1 - lax.axis_index("sec"), lax.axis_index("grp"), lax.axis_index("dev"))
        return remote(
            source.at[rest], target.at[rest], self.sems.at[first], self.sems.at[first + 1], other
        )

    def gather(self):
        me = self.me
        self.bulk(self.stage, self.slots, 0).wait_recv()
        self.slots[me] = self.stage[me]
        self.total[me] = jnp.sum(self.slots[...], axis=0)
        everyone(
            lambda d, where: remote(
                self.total.at[me], self.total.at[me], self.sems.at[2], self.sems.at[3], where
            ).start()
        )

    def finish(self):
        self.bulk(self.total, self.total, 2).wait_recv()
        self.bulk(self.stage, self.slots, 0).wait_send()
        self.bulk(self.total, self.total, 2).wait_send()


def exchange_kernel(
    subdomains, face, x_ref, prior_ref, cross_ref, faces_ref, edge_ref, xs_ref,
    stage, slots, total, sems, face_sems, edge_sems, twin_sems, held, held_sems,
):
    n = 2 * subdomains
    me = own_index()
    sec, g, d = lax.axis_index("sec"), lax.axis_index("grp"), lax.axis_index("dev")
    mine = lax.rem(me, subdomains)
    rows = x_ref.shape[1]
    partners = [
        (0, g, d + 1 - 2 * lax.rem(d, 2)),
        (0, g, d + 2 - 4 * lax.rem(d // 2, 2)),
        (0, g + 1 - 2 * lax.rem(g, 2), d),
        (0, g + 2 - 4 * lax.rem(g // 2, 2), d),
    ]

    def face_copy(m):
        return remote(
            x_ref.at[:, pl.ds(m * face, face)], faces_ref.at[m], face_sems.at[0, m],
            face_sems.at[1, m], partners[m],
        )

    def edge_copy(side):
        to = subdomains + lax.rem(mine + (1 if side == 0 else subdomains - 1), subdomains)
        at = rows - LANES if side == 0 else 0
        return remote(
            x_ref.at[:, pl.ds(at, LANES)], edge_ref.at[side], edge_sems.at[0, side],
            edge_sems.at[1, side], place(to),
        )

    def twin_copy():
        return remote(x_ref, xs_ref, twin_sems.at[0], twin_sems.at[1], (1, g, d))

    chunk = held.shape[1] // held_sems.shape[0]
    incoming = stream(prior_ref, held, held_sems, chunk)
    for i in range(rows // chunk):
        incoming(i).start()
    pl.semaphore_wait(announce(), n - 1)

    @pl.when(sec == 0)
    def _():
        twin_copy().start()
        for m in range(ROUNDS):
            face_copy(m).start()

    @pl.when(sec == 1)
    def _():
        edge_copy(0).start()
        edge_copy(1).start()

    basis = prior_ref.shape[0]

    def product(i, carry):
        same, mixed = carry
        incoming(i).wait()
        hi, lo = split2(held[:, pl.ds(pl.multiple_of(i * chunk, chunk), chunk)])
        return same + nt(hi, hi), mixed + nt(hi, lo)

    zero = jnp.zeros((basis, basis), F32)
    same, mixed = lax.fori_loop(0, rows // chunk, product, (zero, zero))
    part = same + mixed + mixed.T
    piece = basis // n
    stage[...] = part.reshape(n, piece, basis)
    summing = Summing(me, n, stage, slots, total, sems)
    summing.scatter()
    summing.gather()
    summing.finish()
    cross_ref[...] = total[...].reshape(basis, basis)

    @pl.when(sec == 0)
    def _():
        for m in range(ROUNDS):
            face_copy(m).wait()
        twin_copy().wait_send()

    @pl.when(sec == 1)
    def _():
        edge_copy(0).wait()
        edge_copy(1).wait()
        twin_copy().wait_recv()


def finish_kernel(
    subdomains, total_rows, image_ref, prior_ref, cross_ref, next_ref, coef_ref, fac_ref,
    high_ref, low_ref, stage, slots, total, sems, held, held_sems,
):
    n = 2 * subdomains
    me = own_index()
    width, rows = image_ref.shape
    basis = prior_ref.shape[0]
    chunk = held.shape[1] // held_sems.shape[0]
    incoming = stream(prior_ref, held, held_sems, chunk)
    for i in range(rows // chunk):
        incoming(i).start()
    barrier = announce()

    def product(i, carry):
        head, square = carry
        at = pl.ds(pl.multiple_of(i * chunk, chunk), chunk)
        incoming(i).wait()
        hi, lo = split2(held[:, at])
        high_ref[:, at] = hi
        low_ref[:, at] = lo
        ih, il = split2(image_ref[:, at])
        both = nt(jnp.concatenate([ih, il], axis=0), hi)
        head = head + both[:width] + both[width:] + nt(ih, lo)
        mixed = nt(ih, il)
        square = square + nt(ih, ih) + mixed + mixed.T
        return head, square

    head, square = lax.fori_loop(
        0, rows // chunk, product,
        (jnp.zeros((width, basis), F32), jnp.zeros((width, width), F32)),
    )
    part = jnp.concatenate(
        [head, square, jnp.zeros((width, -(basis + width) % LANES), F32)], axis=1
    )
    cuts = n // width
    span = part.shape[1] // cuts
    for i in range(n):
        row, cut = i // cuts, i % cuts
        stage[i] = part[row : row + 1, cut * span : (cut + 1) * span]
    pl.semaphore_wait(barrier, n - 1)
    summing = Summing(me, n, stage, slots, total, sems)
    summing.scatter()
    summing.gather()
    summing.finish()
    lines = [
        jnp.concatenate([total[r * cuts + c] for c in range(cuts)], axis=1) if cuts > 1 else total[r]
        for r in range(width)
    ]
    summed = jnp.concatenate(lines, axis=0)
    first = summed[:, :basis]
    square = summed[:, basis : basis + width]
    cross = cross_ref[...]
    highest = lax.Precision.HIGHEST

    def dot(a, b):
        return jnp.dot(a, b, precision=highest, preferred_element_type=F32)

    def dot_nt(a, b):
        return lax.dot_general(a, b, NT, precision=highest, preferred_element_type=F32)

    coef = 2.0 * first - dot(first, cross)
    gram = (
        square - dot_nt(coef, first) - dot_nt(first, coef) + dot_nt(dot(coef, cross), coef)
    ) * (1.0 / total_rows)
    coef_ref[...] = coef.T
    sub = lax.broadcasted_iota(jnp.int32, (width, 2 * width), 0)
    lane = lax.broadcasted_iota(jnp.int32, (width, 2 * width), 1)
    eye = jnp.where(sub + width == lane, 1.0, 0.0)
    work = jnp.concatenate([gram, jnp.zeros((width, width), F32)], axis=1) + eye
    for j in range(width):
        root = jnp.sqrt(work[j : j + 1, j : j + 1])
        row = work[j : j + 1, :] / root
        column = work[:, j : j + 1] / root
        work = jnp.where(sub == j, row, jnp.where(sub > j, work - column * row, work))
    fac_ref[...] = jnp.where(sub <= lane, work, 0.0)[:, :width]
    inverse = work[:, width:]
    mix = -dot(inverse, coef)
    vh, vl = split2(inverse)
    mh, ml = split2(mix)
    vs = jnp.concatenate([vh, vl], axis=0)
    ms = jnp.concatenate([mh, ml], axis=0)

    def out(i, carry):
        at = pl.ds(pl.multiple_of(i * chunk, chunk), chunk)
        ih, il = split2(image_ref[:, at])
        a = jnp.dot(ms, high_ref[:, at], preferred_element_type=F32)
        a = a + jnp.dot(vs, ih, preferred_element_type=F32)
        c = jnp.dot(mh, low_ref[:, at], preferred_element_type=F32)
        c = c + jnp.dot(vh, il, preferred_element_type=F32)
        next_ref[:, at] = a[:width] + a[width:] + c
        return carry

    lax.fori_loop(0, rows // chunk, out, 0)


def call(kernel, out_shape, *args, scratch=(), ident=None, kept=()):
    multi = isinstance(out_shape, (list, tuple))
    spec = pl.BlockSpec(memory_space=pltpu.VMEM)
    return pl.pallas_call(
        kernel,
        out_shape=out_shape,
        in_specs=[
            pl.BlockSpec(memory_space=pltpu.HBM) if i in kept else spec for i in range(len(args))
        ],
        out_specs=tuple([spec] * len(out_shape)) if multi else spec,
        scratch_shapes=list(scratch),
        compiler_params=pltpu.CompilerParams(
            vmem_limit_bytes=40 << 20, collective_id=ident, has_side_effects=ident is not None
        ),
    )(*args)


def shards(
    current, prior, block_values, block_cols, face_match, face_weight,
    fluid_diag, wet_source, wet_dest, wet_target, wet_weight,
):
    high = lax.Precision.HIGH
    width, local_rows = current.shape
    face_rows = face_match.shape[2]
    row_blocks = block_cols.shape[0]
    wet_slots = wet_source.shape[0]
    grp, dev = lax.axis_size("grp"), lax.axis_size("dev")
    subdomains = grp * dev
    total_rows = local_rows * lax.axis_size("sec") * subdomains
    capacity = 2 * wet_slots // subdomains + 8
    per = -(-capacity // LANES)
    slabs = subdomains * per
    is_shell = lax.axis_index("sec") == 0
    flat_prior = prior.reshape(-1, local_rows)
    basis = flat_prior.shape[0]
    n = 2 * subdomains
    stream_scratch = [
        pltpu.VMEM((basis, local_rows), F32),
        pltpu.SemaphoreType.DMA((local_rows // 1024,)),
    ]
    cross, faces, edges, twin = call(
        functools.partial(exchange_kernel, subdomains, face_rows),
        (
            jax.ShapeDtypeStruct((basis, basis), F32),
            jax.ShapeDtypeStruct((ROUNDS, width, face_rows), F32),
            jax.ShapeDtypeStruct((2, width, LANES), F32),
            jax.ShapeDtypeStruct(current.shape, F32),
        ),
        current, flat_prior,
        scratch=[
            pltpu.VMEM((n, basis // n, basis), F32),
            pltpu.VMEM((n, basis // n, basis), F32),
            pltpu.VMEM((n, basis // n, basis), F32),
            pltpu.SemaphoreType.DMA((4,)),
            pltpu.SemaphoreType.DMA((2, ROUNDS)),
            pltpu.SemaphoreType.DMA((2, 2)),
            pltpu.SemaphoreType.DMA((2,)),
            *stream_scratch,
        ],
        ident=0, kept=(1,),
    )
    tiled = (wet_slots // LANES, LANES)
    bands = local_rows // (2 * LANES) * width
    slab = pltpu.VMEM((slabs, width + META, LANES), F32)
    fluid = call(
        functools.partial(wet_kernel, subdomains, per),
        jax.ShapeDtypeStruct((width, local_rows), F32),
        current, twin, fluid_diag[None, :], edges, wet_source.reshape(tiled),
        wet_dest.reshape(tiled), wet_target.reshape(tiled), wet_weight.reshape(tiled),
        scratch=[
            pltpu.VMEM((4, slabs, LANES), F32),
            slab,
            slab,
            pltpu.VMEM((bands, 2 * per * LANES), BF16),
            pltpu.VMEM((bands, 2 * LANES), F32),
            pltpu.SemaphoreType.DMA((2, subdomains)),
        ],
        ident=2,
    )

    def shell_apply(vector):
        picked = vector.reshape(width, row_blocks, BS)[:, block_cols, :]
        matrices = block_values.reshape(row_blocks, NB, BS, BS)
        result = jnp.einsum("kibc,ibrc->kir", picked, matrices, precision=high)
        return call(
            face_kernel, jax.ShapeDtypeStruct((width, local_rows), F32),
            result.reshape(width, local_rows), faces, face_match[0], face_weight[0],
        )

    image = lax.cond(is_shell, shell_apply, lambda x: fluid, current)
    lanes = -(-(basis + width) // LANES) * LANES
    cuts = n // width
    piece = pltpu.VMEM((n, 1, lanes // cuts), F32)
    next_block, coef, factor = call(
        functools.partial(finish_kernel, subdomains, total_rows),
        (
            jax.ShapeDtypeStruct((width, local_rows), F32),
            jax.ShapeDtypeStruct((basis, width), F32),
            jax.ShapeDtypeStruct((width, width), F32),
        ),
        image, flat_prior, cross,
        scratch=[
            pltpu.VMEM((basis, local_rows), BF16),
            pltpu.VMEM((basis, local_rows), BF16),
            piece, piece, piece,
            pltpu.SemaphoreType.DMA((4,)),
            *stream_scratch,
        ],
        ident=1, kept=(1,),
    )
    return (next_block, coef.reshape(prior.shape[0], width, width), factor)


def solution(mesh):
    placed = (
        P(None, ALL),
        P(None, None, ALL),
        P(("grp", "dev"), None, None),
        P(("grp", "dev"), None),
        P(("grp", "dev"), None, None),
        P(("grp", "dev"), None, None),
        P(("grp", "dev")),
        P(("grp", "dev")),
        P(("grp", "dev"), None),
        P(("grp", "dev")),
        P(("grp", "dev")),
    )
    return jax.shard_map(
        shards, mesh=mesh, in_specs=placed, out_specs=(P(None, ALL), P(), P()), check_vma=False
    )
```
